32 devices in a mesh: dp: 2 (over core), tok: 4 (over y, x), exp: 4 (over z).
Axes of the slice: x: 2, y: 2, z: 4, core: 2. Of those that a mesh axis runs over, the one named last changes fastest.
Arguments:
- tokens: bfloat16 [16, 1024, 1280], P(('dp', 'exp'), 'tok'), parts along dimension 0, may hold values from -64 to 64
- router: bfloat16 [1280, 64], P(None, 'dp'), parts along dimension 1, may hold values from -1 to 1
- image_counts: int32 [16, 16], P(('dp', 'exp')), parts along dimension 0, may hold values from 1 to 64, as said below
- image_offsets: int32 [16, 16], P(('dp', 'exp')), parts along dimension 0, may hold values from 0 to 960, as said below
- expert_in: bfloat16 [32, 1280, 4096], P('exp', None, 'tok'), may hold values from -0.15625 to 0.15625
- expert_out: bfloat16 [32, 4096, 1280], P('exp', 'tok'), may hold values from -0.09375 to 0.09375
Outputs:
- moe_out: bfloat16 [16, 1024, 1280], P(('dp', 'exp'), 'tok'), parts along dimension 0
The draws below stay inside these ranges and needn't reach their ends.
There are 2 independent parts, one for each index of `dp`. The reference program is written for one: setup_inputs(seed, part) draws one part's arguments, and reference() takes and returns one part's arrays. A program takes and returns all parts, laid end to end along the dimension named above; an argument that names none is the same for every part. Nothing has to cross between parts.
Inputs may be any that keep to these rules, and one draw needn't show every extreme that they name: Each image of a sequence covers image_counts positions from its image_offsets; the images of one sequence are disjoint, in order of rising offsets, and lie inside the sequence of 1024 positions; the last image of every sequence has 1024 // 16 positions. `image_offsets`: offsets rise along each sequence; the last image of every sequence ends at the sequence's end.
All inputs are finite; a program needn't handle non-finite values.
Results may differ from the reference program's by a relative error of at most 0.012.
Values may be sent and summed in bfloat16 or wider, within the bound.
No kernel may reach another device: no remote copies, remote signals or barrier semaphores. Data moves between devices by JAX's collectives and lax.ppermute only.
A program may use at most 128 MiB of HBM per device.

```python
import math
import jax
import jax.numpy as jnp
from jax import lax

D = 1280
FF = 4096
IMGS = 16
EXPERTS = 32
SEQS = 8
LEN = 1024


def router_table(key):
    table = 3.0 / math.sqrt(D) * jax.random.normal(jax.random.fold_in(key, 101), (D, EXPERTS), jnp.float32)
    return jnp.clip(table, -1.0, 1.0)


def draw_router(key, part):
    return router_table(key).astype(jnp.bfloat16)


def draw_tokens(key, part):
    base = jax.random.normal(jax.random.fold_in(key, 202), (SEQS, LEN, D), jnp.float32)
    return jnp.clip(base, -64.0, 64.0).astype(jnp.bfloat16)


def image_layout(key):
    widest = LEN // IMGS
    counts = jax.random.randint(jax.random.fold_in(key, 301), (SEQS, IMGS), 1, widest + 1)
    counts = counts.at[:, IMGS - 1].set(widest)
    spare_room = LEN - widest - jnp.sum(counts[:, :IMGS - 1], axis=1, keepdims=True)
    gap_sizes = jax.random.randint(jax.random.fold_in(key, 302), (SEQS, IMGS), 0, spare_room // IMGS + 1)
    offsets = jnp.cumsum(counts + gap_sizes, axis=1) - counts
    offsets = offsets.at[:, IMGS - 1].set(LEN - widest)
    return (counts.astype(jnp.int32), offsets.astype(jnp.int32))


def draw_image_counts(key, part):
    return image_layout(key)[0]


def draw_image_offsets(key, part):
    return image_layout(key)[1]


def level_of(key, extent, shards, low, top_value):
    factor_of, own = 1.0, jax.random.fold_in(key, 6)
    for axis_at, parts in shards:
        steps = jnp.exp(jax.random.uniform(jax.random.fold_in(own, axis_at), (parts,), jnp.float32, low / len(shards), top_value / len(shards)))
        factor_of = factor_of * jnp.repeat(steps, extent[axis_at] // parts).reshape([-1 if axis == axis_at else 1 for axis in range(len(extent))])
    return factor_of


def noise(rng, dims, scale, most, cuts=(), kind=jnp.bfloat16):
    values = jax.random.normal(rng, dims, jnp.float32) * scale
    if len(cuts) > 0:
        values = level_of(rng, dims, cuts, -0.22, 0.18) * values
    return jnp.clip(values, min=-most, max=most).astype(kind)


def setup_inputs(seed: int = 0, part: int = 0) -> dict:
    seeds = jax.random.split(jax.random.key(seed), 7)
    part_splits = jax.random.split(jax.random.fold_in(seeds[6], part), 7)
    tokens = draw_tokens(jax.random.fold_in(jax.random.fold_in(seeds[6], part), 71), part)
    router = draw_router(jax.random.fold_in(jax.random.fold_in(seeds[6], part), 71), part)
    image_counts = draw_image_counts(jax.random.fold_in(jax.random.fold_in(seeds[6], part), 71), part)
    image_offsets = draw_image_offsets(jax.random.fold_in(jax.random.fold_in(seeds[6], part), 71), part)
    expert_in = noise(seeds[4], (EXPERTS, D, FF), D ** -0.5, 0.15625, ((0, 4), (2, 4)))
    expert_out = noise(seeds[5], (EXPERTS, FF, D), FF ** -0.5, 0.09375, ((0, 4), (1, 4)))
    return dict(tokens=tokens, router=router, image_counts=image_counts, image_offsets=image_offsets, expert_in=expert_in, expert_out=expert_out)


def reference(tokens, router, image_counts, image_offsets, expert_in, expert_out):
    positions = jnp.arange(LEN, dtype=jnp.int32)
    image_ends = image_offsets + image_counts
    live_mask = jnp.any((positions[None, :, None] >= image_offsets[:, None, :]) & (positions[None, :, None] < image_ends[:, None, :]), axis=-1)

    def dispatch(inputs):
        token_rows, live_rows = inputs
        logits = jnp.dot(token_rows, router, preferred_element_type=jnp.float32)
        column_peak = jnp.max(jnp.where(live_rows[:, None], logits, -1e30), axis=0)
        weights = jnp.where(live_rows[:, None], jnp.exp(logits - column_peak[None, :]), 0.0)
        totals = jnp.sum(weights, axis=0)
        slot_sums = jnp.dot(weights.astype(jnp.bfloat16).T, token_rows, preferred_element_type=jnp.float32)
        return (slot_sums / totals[:, None]).astype(jnp.bfloat16)

    slot_in = lax.map(dispatch, (tokens, live_mask))

    def expert(inputs):
        slot_rows, first_weight, second_weight = inputs
        hidden = jax.nn.gelu(jnp.dot(slot_rows, first_weight, preferred_element_type=jnp.float32), approximate=False).astype(jnp.bfloat16)
        return jnp.dot(hidden, second_weight, preferred_element_type=jnp.float32).astype(jnp.bfloat16)

    slot_out = jnp.swapaxes(lax.map(expert, (jnp.swapaxes(slot_in, 0, 1), expert_in, expert_out)), 0, 1)

    def combine(inputs):
        token_rows, live_rows, outputs = inputs
        logits = jnp.dot(token_rows, router, preferred_element_type=jnp.float32)
        weights = jax.nn.softmax(logits, axis=-1).astype(jnp.bfloat16)
        mixed_rows = jnp.dot(weights, outputs, preferred_element_type=jnp.float32)
        return jnp.where(live_rows[:, None], mixed_rows, 0.0).astype(jnp.bfloat16)

    return lax.map(combine, (tokens, live_mask, slot_out))
```

```python
import functools

import jax
import jax.numpy as jnp
from jax import lax
from jax.experimental import pallas as pl
from jax.experimental.pallas import tpu as pltpu
from jax.sharding import PartitionSpec as P

BF, F32 = jnp.bfloat16, jnp.float32
STAT = LANES = 128
VM = pl.BlockSpec(memory_space=pltpu.VMEM)
SM = pl.BlockSpec(memory_space=pltpu.SMEM)


def pieces(x):
    hi = x.astype(BF).astype(F32)
    mid = (x - hi).astype(BF).astype(F32)
    low = (x - hi - mid).astype(BF).astype(F32)
    return hi, mid, low


def dispatch_kernel(n_exp, own, counts_ref, offsets_ref, tokens_ref, router_ref, out_ref, logits_ref, sums_ref):
    seqs, block, width = tokens_ref.shape
    slots = router_ref.shape[0]
    me = lax.axis_index("exp")
    where_at = lax.axis_index("tok") * block + lax.broadcasted_iota(jnp.int32, (1, block), 1)
    lane = lax.broadcasted_iota(jnp.int32, (slots, STAT), 1)
    for b in range(seqs):
        live = jnp.zeros((1, block), jnp.int32)
        for i in range(counts_ref.shape[1]):
            low = offsets_ref[b, i]
            inside = (where_at >= low) & (where_at < low + counts_ref[b, i])
            live = jnp.where(inside, 1, live)
        live = live > 0
        tokens = tokens_ref[b]
        logits = lax.dot_general(
            router_ref[...], tokens, (((1,), (1,)), ((), ())), preferred_element_type=F32
        )
        peak = jnp.max(jnp.where(live, logits, -1e30), axis=1, keepdims=True)
        weights = jnp.where(live, jnp.exp(logits - peak), 0.0)
        total = jnp.sum(weights, axis=1, keepdims=True)
        sums_ref[:, :width] = jnp.dot(weights.astype(BF), tokens, preferred_element_type=F32)
        stats = jnp.zeros((slots, STAT), F32)
        for j, part in enumerate(pieces(peak) + pieces(total)):
            stats = jnp.where(lane == j, part, stats)
        sums_ref[:, width:] = stats
        logits_ref[b] = jnp.where(live, logits, -1e30)
        for k in range(n_exp):
            rows = pl.ds(pl.multiple_of(lax.rem(me + k, n_exp) * own, own), own)
            out_ref[k, b * own:(b + 1) * own, :] = sums_ref[rows, :].astype(BF)


def weights_kernel(n_exp, own, logits_ref, out_ref, weights_ref, rel_ref):
    seqs, slots, block = logits_ref.shape
    me = lax.axis_index("exp")
    rel_ref[...] = jnp.zeros_like(rel_ref)
    for b in range(seqs):
        logits = logits_ref[b]
        dead = logits[:1] < -9e29
        grown = jnp.exp(logits - jnp.max(logits, axis=0, keepdims=True))
        weights = grown / jnp.sum(grown, axis=0, keepdims=True)
        weights_ref[...] = jnp.where(dead, 0.0, weights)
        for k in range(n_exp):
            rows = pl.ds(pl.multiple_of(lax.rem(me + k, n_exp) * own, own), own)
            at = (k * seqs + b) * own
            rel_ref[b, at:at + own, :] = weights_ref[rows, :]
    for b in range(seqs):
        out_ref[b] = rel_ref[b].T.astype(BF)


def merge_kernel(n_exp, *refs):
    parts, outs = refs[:-n_exp - 1], refs[-n_exp:]
    width = outs[0].shape[-1]
    for k in range(n_exp):
        stats = [part[k, :, width:].astype(F32) for part in parts]
        peaks = [s[:, 0:1] + s[:, 1:2] + s[:, 2:3] for s in stats]
        totals = [s[:, 3:4] + s[:, 4:5] + s[:, 5:6] for s in stats]
        top = functools.reduce(jnp.maximum, peaks)
        scales = [jnp.exp(peak - top) for peak in peaks]
        total = sum(t * s for t, s in zip(totals, scales))
        sums = sum(part[k, :, :width].astype(F32) * s for part, s in zip(parts, scales))
        outs[k][...] = (sums / total).astype(BF)


def expert_kernel(n_exp, own, *refs):
    slots = refs[:n_exp]
    first_ref, second_ref, out_ref, in_ref, sum_ref = refs[n_exp:]
    rows = slots[0].shape[0]
    chunks = in_ref.shape[0]
    for k in range(n_exp):
        for c in range(chunks):
            in_ref[c, k * rows:(k + 1) * rows, :] = slots[k][:, c * LANES:(c + 1) * LANES].astype(F32)
    count = n_exp * rows // own
    for s in range(own):
        same = pl.ds(s, count, stride=own)
        mine = jnp.concatenate([in_ref[c, same, :] for c in range(chunks)], axis=1).astype(BF)
        hidden = jnp.dot(mine, first_ref[s], preferred_element_type=F32)
        hidden = (0.5 * hidden * (1.0 + lax.erf(hidden * 0.7071067811865476))).astype(BF)
        partial = jnp.dot(hidden, second_ref[s], preferred_element_type=F32)
        for c in range(chunks):
            sum_ref[c, same, :] = partial[:, c * LANES:(c + 1) * LANES]
    for k in range(n_exp):
        for c in range(chunks):
            out_ref[k][:, c * LANES:(c + 1) * LANES] = sum_ref[c, k * rows:(k + 1) * rows, :].astype(BF)


def combine_kernel(*refs):
    weights_ref, out_ref, parts = refs[0], refs[-1], refs[1:-1]
    slot_out = sum(part[...].astype(F32) for part in parts).astype(BF)
    for b in range(out_ref.shape[0]):
        out_ref[b] = jnp.dot(weights_ref[b], slot_out, preferred_element_type=F32).astype(BF)


def call(kernel, outs, scratch, limit, flops=0, moved=0):
    return pl.pallas_call(
        kernel,
        out_shape=outs,
        scratch_shapes=scratch,
        compiler_params=pltpu.CompilerParams(vmem_limit_bytes=limit),
        cost_estimate=pl.CostEstimate(flops=flops, bytes_accessed=moved, transcendentals=0),
    )


def shards(tokens, router, image_counts, image_offsets, expert_in, expert_out):
    n_tok, n_exp = lax.axis_size("tok"), lax.axis_size("exp")
    seqs, block, width = tokens.shape
    slots, own = router.shape[1], expert_in.shape[0]
    rows = seqs * own
    S = jax.ShapeDtypeStruct
    limit = max(4 << 20, 8 * n_tok * n_exp * rows * (width + STAT))

    def exchange(x, axis, n, k):
        return lax.ppermute(x, axis, [(i, (i + k) % n) for i in range(n)])

    def gather_tok(x):
        return [x] + [exchange(x, "tok", n_tok, k) for k in range(1, n_tok)]

    parts, logits = pl.pallas_call(
        functools.partial(dispatch_kernel, n_exp, own),
        in_specs=[SM, SM, VM, VM],
        out_shape=[S((n_exp, rows, width + STAT), BF), S((seqs, slots, block), F32)],
        scratch_shapes=[pltpu.VMEM((slots, width + STAT), F32)],
        compiler_params=pltpu.CompilerParams(vmem_limit_bytes=4 << 20),
        cost_estimate=pl.CostEstimate(flops=COST_A, bytes_accessed=0, transcendentals=0),
    )(image_counts, image_offsets, tokens, router.T)
    gathered = gather_tok(parts)
    combine_weights = call(
        functools.partial(weights_kernel, n_exp, own),
        S((seqs, block, n_exp * rows), BF),
        [pltpu.VMEM((slots, block), F32), pltpu.VMEM((seqs, n_exp * rows, block), F32)],
        4 << 20,
        COST_W,
    )(logits)
    merged = call(
        functools.partial(merge_kernel, n_exp), [S((rows, width), BF)] * n_exp, [], limit, COST_M
    )(*gathered, combine_weights)
    arrived = [merged[0]] + [exchange(merged[k], "exp", n_exp, k) for k in range(1, n_exp)]
    partial = call(
        functools.partial(expert_kernel_flat, n_exp, own),
        [S((rows, width), BF)] * n_exp,
        [pltpu.VMEM((width // LANES, n_exp * rows, LANES), F32)] * 2,
        EXPERT_LIMIT,
    )(*arrived, expert_in, expert_out)
    returned = [partial[0]] + [exchange(partial[k], "exp", n_exp, n_exp - k) for k in range(1, n_exp)]
    gathered_out = gather_tok(jnp.concatenate(returned, axis=0))
    return call(combine_kernel, S(tokens.shape, BF), [], limit)(combine_weights, *gathered_out)


EXPERT_LIMIT = 8 << 20
COST_A = 0_000_000_000
COST_W = 10_000_000_000
COST_M = 6_000_000_000


def expert_kernel_flat(n_exp, own, *refs):
    ins, outs, scratch = refs[:n_exp + 2], refs[n_exp + 2:2 * n_exp + 2], refs[2 * n_exp + 2:]
    expert_kernel(n_exp, own, *ins, outs, *scratch)


def solution(mesh):
    placed = (
        P(("dp", "exp"), "tok", None),
        P(None, "dp"),
        P(("dp", "exp"), None),
        P(("dp", "exp"), None),
        P("exp", None, "tok"),
        P("exp", "tok", None),
    )
    return jax.shard_map(
        shards, mesh=mesh, in_specs=placed, out_specs=P(("dp", "exp"), "tok", None), check_vma=False
    )
```

```python
import functools

import jax
import jax.numpy as jnp
from jax import lax
from jax.experimental import pallas as pl
from jax.experimental.pallas import tpu as pltpu
from jax.sharding import PartitionSpec as P

BF, F32 = jnp.bfloat16, jnp.float32
STAT = LANES = 128
VM = pl.BlockSpec(memory_space=pltpu.VMEM)
ANY = pl.BlockSpec(memory_space=pl.ANY)
WHOLE = 8 << 20


TOK_XOR, EXP_XOR = True, True
TOK_ORDER, TOK2_ORDER = 1, 1
GROUPS = lambda n: [list(range(1, n)), [0]]


def peer(i, k, n):
    if EXP_XOR:
        return i ^ k
    return (i + k) % n if isinstance(i, int) else lax.rem(i + k, n)


def tok_peer(i, k, n):
    return i ^ k if TOK_XOR else (i + k) % n


def pieces(x):
    hi = x.astype(BF).astype(F32)
    mid = (x - hi).astype(BF).astype(F32)
    low = (x - hi - mid).astype(BF).astype(F32)
    return hi, mid, low


def dispatch_kernel(
    n_exp, own, groups, counts_hbm, offsets_hbm, tokens_hbm, router_hbm, *refs
):
    out_refs, logits_ref = refs[:len(groups)], refs[len(groups)]
    counts_ref, offsets_ref, tokens_ref, router_ref, sums_ref, done = refs[len(groups) + 1:]
    seqs, block, width = tokens_ref.shape
    slots = router_ref.shape[0]
    copies = [
        pltpu.make_async_copy(source, target, done.at[i])
        for i, (source, target) in enumerate(
            [(tokens_hbm.at[0], tokens_ref.at[0]), (router_hbm, router_ref)]
            + [(counts_hbm, counts_ref), (offsets_hbm, offsets_ref)]
            + [(tokens_hbm.at[b], tokens_ref.at[b]) for b in range(1, seqs)]
        )
    ]
    for copy in copies:
        copy.start()
    me = lax.axis_index("exp")
    where_at = lax.axis_index("tok") * block + lax.broadcasted_iota(jnp.int32, (1, block), 1)
    lane = lax.broadcasted_iota(jnp.int32, (slots, STAT), 1)
    for copy in copies[2:4]:
        copy.wait()
    lives = []
    for b in range(seqs):
        live = jnp.zeros((1, block), jnp.int32)
        for i in range(counts_ref.shape[1]):
            low = offsets_ref[b, i]
            inside = (where_at >= low) & (where_at < low + counts_ref[b, i])
            live = jnp.where(inside, 1, live)
        lives.append(live > 0)
    for copy in copies[:2]:
        copy.wait()
    for b in range(seqs):
        if b > 0:
            copies[3 + b].wait()
        live = lives[b]
        tokens = tokens_ref[b]
        logits = lax.dot_general(
            router_ref[...], tokens, (((1,), (1,)), ((), ())), preferred_element_type=F32
        )
        masked = jnp.where(live, logits, -1e30)
        peak = jnp.max(masked, axis=1, keepdims=True)
        weights = jnp.where(live, jnp.exp(masked - peak), 0.0)
        total = jnp.sum(weights, axis=1, keepdims=True)
        sums_ref[:, :width] = jnp.dot(weights.astype(BF), tokens, preferred_element_type=F32)
        stats = jnp.zeros((slots, STAT), F32)
        for j, part in enumerate(pieces(peak) + pieces(total)):
            stats = jnp.where(lane == j, part, stats)
        sums_ref[:, width:] = stats
        logits_ref[b] = masked
        for out_ref, group in zip(out_refs, groups):
            for j, k in enumerate(group):
                rows = pl.ds(pl.multiple_of(peer(me, k, n_exp) * own, own), own)
                out_ref[j, b * own:(b + 1) * own, :] = sums_ref[rows, :].astype(BF)


def weights_kernel(n_exp, own, logits_ref, part_ref, out_ref, part_out_ref, weights_ref, rel_ref):
    part_out_ref[...] = part_ref[...]
    seqs, slots, block = logits_ref.shape
    me = lax.axis_index("exp")
    rel_ref[...] = jnp.zeros_like(rel_ref)
    for b in range(seqs):
        logits = logits_ref[b]
        dead = logits[:1] < -9e29
        grown = jnp.exp(logits - jnp.max(logits, axis=0, keepdims=True))
        weights = grown / jnp.sum(grown, axis=0, keepdims=True)
        weights_ref[...] = jnp.where(dead, 0.0, weights)
        for k in range(n_exp):
            rows = pl.ds(pl.multiple_of(peer(me, k, n_exp) * own, own), own)
            at = (k * seqs + b) * own
            rel_ref[b, at:at + own, :] = weights_ref[rows, :]
    for b in range(seqs):
        out_ref[b] = rel_ref[b].T.astype(BF)


def merge_kernel(n_exp, *refs):
    parts, outs = refs[:-n_exp - 1], refs[-n_exp:]
    width = outs[0].shape[-1]
    for k in range(n_exp):
        stats = [part[k, :, width:].astype(F32) for part in parts]
        peaks = [s[:, 0:1] + s[:, 1:2] + s[:, 2:3] for s in stats]
        totals = [s[:, 3:4] + s[:, 4:5] + s[:, 5:6] for s in stats]
        top = functools.reduce(jnp.maximum, peaks)
        scales = [jnp.exp(peak - top) for peak in peaks]
        total = sum(t * s for t, s in zip(totals, scales))
        sums = sum(part[k, :, :width].astype(F32) * s for part, s in zip(parts, scales))
        outs[k][...] = (sums / total).astype(BF)


def expert_kernel(n_exp, own, groups, *refs):
    slots = refs[:n_exp]
    first_ref, second_ref, out_ref, in_ref, sum_ref = refs[n_exp:]
    rows = slots[0].shape[0]
    chunks = in_ref.shape[0]
    for k in range(n_exp):
        for c in range(chunks):
            in_ref[c, k * rows:(k + 1) * rows, :] = slots[k][:, c * LANES:(c + 1) * LANES].astype(F32)
    count = n_exp * rows // own
    for s in range(own):
        same = pl.ds(s, count, stride=own)
        mine = jnp.concatenate([in_ref[c, same, :] for c in range(chunks)], axis=1).astype(BF)
        hidden = jnp.dot(mine, first_ref[s], preferred_element_type=F32)
        hidden = (0.5 * hidden * (1.0 + lax.erf(hidden * 0.7071067811865476))).astype(BF)
        partial = jnp.dot(hidden, second_ref[s], preferred_element_type=F32)
        for c in range(chunks):
            sum_ref[c, same, :] = partial[:, c * LANES:(c + 1) * LANES]
    for ref, group in zip(out_ref, groups):
        for j, k in enumerate(group):
            for c in range(chunks):
                ref[j, :, c * LANES:(c + 1) * LANES] = sum_ref[c, k * rows:(k + 1) * rows, :].astype(BF)


def total_kernel(*refs):
    n = refs[0].shape[0]
    parts, outs = refs[:-n], refs[-n:]
    for k in range(n):
        outs[k][...] = sum(part[k].astype(F32) for part in parts).astype(BF)


def copy_kernel(in_ref, out_ref):
    out_ref[...] = in_ref[...]


def combine_kernel(*refs):
    weights_ref, out_hbm, out_ref, done, parts = refs[0], refs[-3], refs[-2], refs[-1], refs[1:-3]
    seqs, block, _ = out_ref.shape
    step = block // 2
    slot_out = jnp.concatenate([part[...] for part in parts], axis=0)
    copies = []
    for b in range(seqs):
        for j in range(2):
            rows = slice(j * step, (j + 1) * step)
            mixed = jnp.dot(weights_ref[b, rows, :], slot_out, preferred_element_type=F32)
            out_ref[b, rows, :] = mixed.astype(BF)
            at = b * 2 + j
            copies.append(pltpu.make_async_copy(out_ref.at[b, rows], out_hbm.at[b, rows], done.at[at]))
            copies[-1].start()
    for copy in copies:
        copy.wait()


def call(kernel, outs, scratch, limit, flops=0, moved=0):
    return pl.pallas_call(
        kernel,
        out_shape=outs,
        scratch_shapes=scratch,
        compiler_params=pltpu.CompilerParams(vmem_limit_bytes=limit),
        cost_estimate=pl.CostEstimate(flops=flops, bytes_accessed=moved, transcendentals=0),
    )


def shards(tokens, router, image_counts, image_offsets, expert_in, expert_out):
    n_tok, n_exp = lax.axis_size("tok"), lax.axis_size("exp")
    seqs, block, width = tokens.shape
    slots, own = router.shape[1], expert_in.shape[0]
    rows = seqs * own
    S = jax.ShapeDtypeStruct
    limit = max(4 << 20, 8 * n_tok * n_exp * rows * (width + STAT))

    def gather_tok(x, order):
        got = {}
        for k in list(range(1, n_tok))[::order]:
            got[k] = lax.ppermute(x, "tok", [(i, tok_peer(i, k, n_tok)) for i in range(n_tok)])
        return [x] + [got[k] for k in range(1, n_tok)]

    def send(x, k, back):
        if k == 0:
            return x
        pairs = [(i, peer(i, k, n_exp)) for i in range(n_exp)]
        return lax.ppermute(x, "exp", [(b, a) for a, b in pairs] if back else pairs)

    groups = GROUPS(n_exp)
    *parts, logits = pl.pallas_call(
        functools.partial(dispatch_kernel, n_exp, own, groups),
        in_specs=[pl.BlockSpec(memory_space=pltpu.HBM)] * 4,
        out_shape=[S((len(g), rows, width + STAT), BF) for g in groups] + [S((seqs, slots, block), F32)],
        scratch_shapes=[
            pltpu.SMEM(image_counts.shape, jnp.int32),
            pltpu.SMEM(image_offsets.shape, jnp.int32),
            pltpu.VMEM(tokens.shape, BF),
            pltpu.VMEM((slots, width), BF),
            pltpu.VMEM((slots, width + STAT), F32),
            pltpu.SemaphoreType.DMA((seqs + 3,)),
        ],
        compiler_params=pltpu.CompilerParams(vmem_limit_bytes=WHOLE),
        cost_estimate=pl.CostEstimate(flops=COST_A, bytes_accessed=0, transcendentals=0),
    )(*[pltpu.with_memory_space_constraint(x, pltpu.HBM) for x in (image_counts, image_offsets, tokens, router.T)])
    gathered = [gather_tok(part, TOK_ORDER) for part in parts[:-1]]
    combine_weights, parts[-1] = call(
        functools.partial(weights_kernel, n_exp, own),
        [S((seqs, block, n_exp * rows), BF), S(parts[-1].shape, BF)],
        [pltpu.VMEM((slots, block), F32), pltpu.VMEM((seqs, n_exp * rows, block), F32)],
        4 << 20,
        COST_W,
    )(logits, parts[-1])
    gathered.append(gather_tok(parts[-1], TOK_ORDER))
    arrived = {}
    for group, part in zip(groups, gathered):
        merged = call(
            functools.partial(merge_kernel, len(group)),
            [S((rows, width), BF)] * len(group), [], limit, COST_M,
        )(*part, combine_weights)
        for k, block in zip(group, merged):
            arrived[k] = send(block, k, False)
    arrived = [arrived[k] for k in range(n_exp)]
    partial = call(
        functools.partial(expert_kernel_flat, n_exp, own, groups),
        [S((len(g), rows, width), BF) for g in groups],
        [pltpu.VMEM((width // LANES, n_exp * rows, LANES), F32)] * 2,
        EXPERT_LIMIT,
    )(*arrived, expert_in, expert_out)
    gathered = [gather_tok(part, TOK2_ORDER) for part in partial[:-1]]
    mine = call(copy_kernel, S(partial[-1].shape, BF), [], 1 << 20, COST_C)(partial[-1])
    gathered.append(gather_tok(mine, TOK2_ORDER))
    returned = {}
    for group, part in zip(groups, gathered):
        totals = call(total_kernel, [S((rows, width), BF)] * len(group), [], limit)(*part)
        for k, block_out in zip(group, totals):
            returned[k] = send(block_out, k, True)
    return pl.pallas_call(
        combine_kernel,
        in_specs=[VM] * (1 + n_exp),
        out_specs=ANY,
        out_shape=S(tokens.shape, BF),
        scratch_shapes=[pltpu.VMEM(tokens.shape, BF), pltpu.SemaphoreType.DMA((2 * seqs,))],
        compiler_params=pltpu.CompilerParams(vmem_limit_bytes=limit + (4 << 20)),
    )(combine_weights, *[returned[k] for k in range(n_exp)])


EXPERT_LIMIT = 8 << 20
COST_C = 3_000_000_000
COST_A = 40_000_000_000
COST_W = 6_000_000_000
COST_M = 0_000_000_000


def expert_kernel_flat(n_exp, own, groups, *refs):
    n = len(groups)
    ins, outs, scratch = refs[:n_exp + 2], refs[n_exp + 2:n_exp + 2 + n], refs[n_exp + 2 + n:]
    expert_kernel(n_exp, own, groups, *ins, outs, *scratch)


def solution(mesh):
    placed = (
        P(("dp", "exp"), "tok", None),
        P(None, "dp"),
        P(("dp", "exp"), None),
        P(("dp", "exp"), None),
        P("exp", None, "tok"),
        P("exp", "tok", None),
    )
    return jax.shard_map(
        shards, mesh=mesh, in_specs=placed, out_specs=P(("dp", "exp"), "tok", None), check_vma=False
    )
```

```python
import functools

import jax
import jax.numpy as jnp
from jax import lax
from jax.experimental import pallas as pl
from jax.experimental.pallas import tpu as pltpu
from jax.sharding import PartitionSpec as P

BF, F32 = jnp.bfloat16, jnp.float32
STAT = LANES = 128
VM = pl.BlockSpec(memory_space=pltpu.VMEM)
ANY = pl.BlockSpec(memory_space=pl.ANY)
WHOLE = 8 << 20


EXP_STEPS = (0, 3, 1, 2)
TOK_STEPS = (0, 2, 1, 3)
TOK_ORDER, TOK2_ORDER = 1, 1
GROUPS = lambda n: [list(range(1, n)), [0]]


def step(k, steps):
    return steps[k] if k < len(steps) else k


def peer(i, k, n):
    return i ^ step(k, EXP_STEPS)


def tok_peer(i, k, n):
    return i ^ step(k, TOK_STEPS)


def pieces(x):
    hi = x.astype(BF).astype(F32)
    mid = (x - hi).astype(BF).astype(F32)
    low = (x - hi - mid).astype(BF).astype(F32)
    return hi, mid, low


def dispatch_kernel(
    n_exp, own, groups, counts_hbm, offsets_hbm, tokens_hbm, router_hbm, *refs
):
    out_refs, logits_ref = refs[:len(groups)], refs[len(groups)]
    counts_ref, offsets_ref, tokens_ref, router_ref, sums_ref, done = refs[len(groups) + 1:]
    seqs, block, width = tokens_ref.shape
    slots = router_ref.shape[0]
    pairs = [(counts_hbm, counts_ref), (offsets_hbm, offsets_ref), (router_hbm, router_ref)]
    pairs += [(tokens_hbm.at[b], tokens_ref.at[b]) for b in range(seqs)]
    copies = [
        pltpu.make_async_copy(source, target, done.at[i]) for i, (source, target) in enumerate(pairs)
    ]
    for copy in copies:
        copy.start()
    me = lax.axis_index("exp")
    where_at = lax.axis_index("tok") * block + lax.broadcasted_iota(jnp.int32, (1, block), 1)
    lane = lax.broadcasted_iota(jnp.int32, (slots, STAT), 1)
    for copy in copies[:2]:
        copy.wait()
    lives = []
    for b in range(seqs):
        live = jnp.zeros((1, block), jnp.int32)
        for i in range(counts_ref.shape[1]):
            low = offsets_ref[b, i]
            inside = (where_at >= low) & (where_at < low + counts_ref[b, i])
            live = jnp.where(inside, 1, live)
        lives.append(live > 0)
    for copy in copies[2:]:
        copy.wait()
    logits = [
        lax.dot_general(
            router_ref[...], tokens_ref[b], (((1,), (1,)), ((), ())), preferred_element_type=F32
        )
        for b in range(seqs)
    ]
    for b in range(seqs):
        live = lives[b]
        masked = jnp.where(live, logits[b], -1e30)
        peak = jnp.max(masked, axis=1, keepdims=True)
        weights = jnp.where(live, jnp.exp(masked - peak), 0.0)
        total = jnp.sum(weights, axis=1, keepdims=True)
        sums_ref[b, :, :width] = jnp.dot(
            weights.astype(BF), tokens_ref[b], preferred_element_type=F32
        )
        stats = jnp.zeros((slots, STAT), F32)
        for j, part in enumerate(pieces(peak) + pieces(total)):
            stats = jnp.where(lane == j, part, stats)
        sums_ref[b, :, width:] = stats
        logits_ref[b] = masked
    for b in range(seqs):
        for out_ref, group in zip(out_refs, groups):
            for j, k in enumerate(group):
                rows = pl.ds(pl.multiple_of(peer(me, k, n_exp) * own, own), own)
                out_ref[j, b * own:(b + 1) * own, :] = sums_ref[b, rows, :].astype(BF)


def weights_kernel(n_exp, own, logits_ref, part_ref, out_ref, part_out_ref, weights_ref, rel_ref):
    part_out_ref[...] = part_ref[...]
    seqs, slots, block = logits_ref.shape
    me = lax.axis_index("exp")
    rel_ref[...] = jnp.zeros_like(rel_ref)
    for b in range(seqs):
        logits = logits_ref[b]
        dead = logits[:1] < -9e29
        grown = jnp.exp(logits - jnp.max(logits, axis=0, keepdims=True))
        weights = grown / jnp.sum(grown, axis=0, keepdims=True)
        weights_ref[...] = jnp.where(dead, 0.0, weights)
        for k in range(n_exp):
            rows = pl.ds(pl.multiple_of(peer(me, k, n_exp) * own, own), own)
            at = (k * seqs + b) * own
            rel_ref[b, at:at + own, :] = weights_ref[rows, :]
    for b in range(seqs):
        out_ref[b] = rel_ref[b].T.astype(BF)


def merge_kernel(n_exp, *refs):
    parts, outs = refs[:-n_exp - 1], refs[-n_exp:]
    width = outs[0].shape[-1]
    for k in range(n_exp):
        stats = [part[k, :, width:].astype(F32) for part in parts]
        peaks = [s[:, 0:1] + s[:, 1:2] + s[:, 2:3] for s in stats]
        totals = [s[:, 3:4] + s[:, 4:5] + s[:, 5:6] for s in stats]
        top = functools.reduce(jnp.maximum, peaks)
        scales = [jnp.exp(peak - top) for peak in peaks]
        total = sum(t * s for t, s in zip(totals, scales))
        sums = sum(part[k, :, :width].astype(F32) * s for part, s in zip(parts, scales))
        outs[k][...] = (sums / total).astype(BF)


def expert_kernel(n_exp, own, groups, *refs):
    slots = refs[:n_exp]
    first_ref, second_ref, out_ref, in_ref, sum_ref = refs[n_exp:]
    rows = slots[0].shape[0]
    chunks = in_ref.shape[0]
    for k in range(n_exp):
        for c in range(chunks):
            in_ref[c, k * rows:(k + 1) * rows, :] = slots[k][:, c * LANES:(c + 1) * LANES].astype(F32)
    count = n_exp * rows // own
    for s in range(own):
        same = pl.ds(s, count, stride=own)
        mine = jnp.concatenate([in_ref[c, same, :] for c in range(chunks)], axis=1).astype(BF)
        hidden = jnp.dot(mine, first_ref[s], preferred_element_type=F32)
        hidden = (0.5 * hidden * (1.0 + lax.erf(hidden * 0.7071067811865476))).astype(BF)
        partial = jnp.dot(hidden, second_ref[s], preferred_element_type=F32)
        for c in range(chunks):
            sum_ref[c, same, :] = partial[:, c * LANES:(c + 1) * LANES]
    for ref, group in zip(out_ref, groups):
        for j, k in enumerate(group):
            for c in range(chunks):
                ref[j, :, c * LANES:(c + 1) * LANES] = sum_ref[c, k * rows:(k + 1) * rows, :].astype(BF)


def total_kernel(*refs):
    n = refs[0].shape[0]
    parts, outs = refs[:-n], refs[-n:]
    for k in range(n):
        outs[k][...] = sum(part[k].astype(F32) for part in parts).astype(BF)


def copy_kernel(in_ref, out_ref):
    out_ref[...] = in_ref[...]


def combine_kernel(*refs):
    weights_ref, out_hbm, out_ref, done, parts = refs[0], refs[-3], refs[-2], refs[-1], refs[1:-3]
    seqs, block, _ = out_ref.shape
    step = block // 2
    slot_out = jnp.concatenate([part[...] for part in parts], axis=0)
    copies = []
    for b in range(seqs):
        for j in range(2):
            rows = slice(j * step, (j + 1) * step)
            mixed = jnp.dot(weights_ref[b, rows, :], slot_out, preferred_element_type=F32)
            out_ref[b, rows, :] = mixed.astype(BF)
            at = b * 2 + j
            copies.append(pltpu.make_async_copy(out_ref.at[b, rows], out_hbm.at[b, rows], done.at[at]))
            copies[-1].start()
    for copy in copies:
        copy.wait()


def call(kernel, outs, scratch, limit, flops=0, moved=0):
    return pl.pallas_call(
        kernel,
        out_shape=outs,
        scratch_shapes=scratch,
        compiler_params=pltpu.CompilerParams(vmem_limit_bytes=limit),
        cost_estimate=pl.CostEstimate(flops=flops, bytes_accessed=moved, transcendentals=0),
    )


def shards(tokens, router, image_counts, image_offsets, expert_in, expert_out):
    n_tok, n_exp = lax.axis_size("tok"), lax.axis_size("exp")
    seqs, block, width = tokens.shape
    slots, own = router.shape[1], expert_in.shape[0]
    rows = seqs * own
    S = jax.ShapeDtypeStruct
    limit = max(4 << 20, 8 * n_tok * n_exp * rows * (width + STAT))

    def gather_tok(x, order):
        got = {}
        for k in list(range(1, n_tok))[::order]:
            got[k] = lax.ppermute(x, "tok", [(i, tok_peer(i, k, n_tok)) for i in range(n_tok)])
        return [x] + [got[k] for k in range(1, n_tok)]

    def send(x, k, back):
        if k == 0:
            return x
        pairs = [(i, peer(i, k, n_exp)) for i in range(n_exp)]
        return lax.ppermute(x, "exp", [(b, a) for a, b in pairs] if back else pairs)

    groups = GROUPS(n_exp)
    *parts, logits = pl.pallas_call(
        functools.partial(dispatch_kernel, n_exp, own, groups),
        in_specs=[pl.BlockSpec(memory_space=pltpu.HBM)] * 4,
        out_shape=[S((len(g), rows, width + STAT), BF) for g in groups] + [S((seqs, slots, block), F32)],
        scratch_shapes=[
            pltpu.SMEM(image_counts.shape, jnp.int32),
            pltpu.SMEM(image_offsets.shape, jnp.int32),
            pltpu.VMEM(tokens.shape, BF),
            pltpu.VMEM((slots, width), BF),
            pltpu.VMEM((seqs, slots, width + STAT), F32),
            pltpu.SemaphoreType.DMA((seqs + 3,)),
        ],
        compiler_params=pltpu.CompilerParams(vmem_limit_bytes=WHOLE),
        cost_estimate=pl.CostEstimate(flops=COST_A, bytes_accessed=0, transcendentals=0),
    )(*[pltpu.with_memory_space_constraint(x, pltpu.HBM) for x in (image_counts, image_offsets, tokens, router.T)])
    gathered = [gather_tok(part, TOK_ORDER) for part in parts[:-1]]
    combine_weights, parts[-1] = call(
        functools.partial(weights_kernel, n_exp, own),
        [S((seqs, block, n_exp * rows), BF), S(parts[-1].shape, BF)],
        [pltpu.VMEM((slots, block), F32), pltpu.VMEM((seqs, n_exp * rows, block), F32)],
        4 << 20,
        COST_W,
    )(logits, parts[-1])
    gathered.append(gather_tok(parts[-1], TOK_ORDER))
    arrived = {}
    for group, part in zip(groups, gathered):
        merged = call(
            functools.partial(merge_kernel, len(group)),
            [S((rows, width), BF)] * len(group), [], limit, COST_M,
        )(*part, combine_weights)
        for k, block in zip(group, merged):
            arrived[k] = send(block, k, False)
    arrived = [arrived[k] for k in range(n_exp)]
    partial = call(
        functools.partial(expert_kernel_flat, n_exp, own, groups),
        [S((len(g), rows, width), BF) for g in groups],
        [pltpu.VMEM((width // LANES, n_exp * rows, LANES), F32)] * 2,
        EXPERT_LIMIT,
    )(*arrived, expert_in, expert_out)
    gathered = [gather_tok(part, TOK2_ORDER) for part in partial[:-1]]
    mine = call(copy_kernel, S(partial[-1].shape, BF), [], 1 << 20, COST_C)(partial[-1])
    gathered.append(gather_tok(mine, TOK2_ORDER))
    returned = {}
    for group, part in zip(groups, gathered):
        totals = call(total_kernel, [S((rows, width), BF)] * len(group), [], limit)(*part)
        for k, block_out in zip(group, totals):
            returned[k] = send(block_out, k, True)
    return pl.pallas_call(
        combine_kernel,
        in_specs=[VM] * (1 + n_exp),
        out_specs=ANY,
        out_shape=S(tokens.shape, BF),
        scratch_shapes=[pltpu.VMEM(tokens.shape, BF), pltpu.SemaphoreType.DMA((2 * seqs,))],
        compiler_params=pltpu.CompilerParams(vmem_limit_bytes=limit + (4 << 20)),
    )(combine_weights, *[returned[k] for k in range(n_exp)])


EXPERT_LIMIT = 8 << 20
COST_C = 3_000_000_000
COST_A = 40_000_000_000
COST_W = 6_000_000_000
COST_M = 0_000_000_000


def expert_kernel_flat(n_exp, own, groups, *refs):
    n = len(groups)
    ins, outs, scratch = refs[:n_exp + 2], refs[n_exp + 2:n_exp + 2 + n], refs[n_exp + 2 + n:]
    expert_kernel(n_exp, own, groups, *ins, outs, *scratch)


def solution(mesh):
    placed = (
        P(("dp", "exp"), "tok", None),
        P(None, "dp"),
        P(("dp", "exp"), None),
        P(("dp", "exp"), None),
        P("exp", None, "tok"),
        P("exp", "tok", None),
    )
    return jax.shard_map(
        shards, mesh=mesh, in_specs=placed, out_specs=P(("dp", "exp"), "tok", None), check_vma=False
    )
```

```python
import functools

import jax
import jax.numpy as jnp
from jax import lax
from jax.experimental import pallas as pl
from jax.experimental.pallas import tpu as pltpu
from jax.sharding import PartitionSpec as P

BF, F32 = jnp.bfloat16, jnp.float32
STAT = LANES = 128
VM = pl.BlockSpec(memory_space=pltpu.VMEM)
ANY = pl.BlockSpec(memory_space=pl.ANY)
WHOLE = 8 << 20


EXP_STEPS = (0, 3, 1, 2)
TOK_STEPS = (0, 2, 1, 3)
TOK_ORDER, TOK2_ORDER = 1, 1
GROUPS = lambda n: [list(range(1, n)), [0]]


def step(k, steps):
    return steps[k] if k < len(steps) else k


def peer(i, k, n):
    return i ^ step(k, EXP_STEPS)


def tok_peer(i, k, n):
    return i ^ step(k, TOK_STEPS)


def pieces(x):
    hi = x.astype(BF).astype(F32)
    mid = (x - hi).astype(BF).astype(F32)
    low = (x - hi - mid).astype(BF).astype(F32)
    return hi, mid, low


def dispatch_kernel(
    n_exp, own, groups, counts_hbm, offsets_hbm, tokens_hbm, router_hbm, *refs
):
    out_refs, logits_ref = refs[:len(groups)], refs[len(groups)]
    counts_ref, offsets_ref, tokens_ref, router_ref, sums_ref, done = refs[len(groups) + 1:]
    seqs, block, width = tokens_ref.shape
    slots = router_ref.shape[0]
    pairs = [(counts_hbm, counts_ref), (offsets_hbm, offsets_ref), (router_hbm, router_ref)]
    pairs += [(tokens_hbm.at[b], tokens_ref.at[b]) for b in range(seqs)]
    copies = [
        pltpu.make_async_copy(source, target, done.at[i]) for i, (source, target) in enumerate(pairs)
    ]
    for copy in copies:
        copy.start()
    me = lax.axis_index("exp")
    where_at = lax.axis_index("tok") * block + lax.broadcasted_iota(jnp.int32, (1, block), 1)
    lane = lax.broadcasted_iota(jnp.int32, (slots, STAT), 1)
    for copy in copies[:2]:
        copy.wait()
    lives = []
    for b in range(seqs):
        live = jnp.zeros((1, block), jnp.int32)
        for i in range(counts_ref.shape[1]):
            low = offsets_ref[b, i]
            inside = (where_at >= low) & (where_at < low + counts_ref[b, i])
            live = jnp.where(inside, 1, live)
        lives.append(live > 0)
    for copy in copies[2:]:
        copy.wait()
    logits = [
        lax.dot_general(
            router_ref[...], tokens_ref[b], (((1,), (1,)), ((), ())), preferred_element_type=F32
        )
        for b in range(seqs)
    ]
    for b in range(seqs):
        live = lives[b]
        masked = jnp.where(live, logits[b], -1e30)
        peak = jnp.max(masked, axis=1, keepdims=True)
        weights = jnp.where(live, jnp.exp(masked - peak), 0.0)
        total = jnp.sum(weights, axis=1, keepdims=True)
        sums_ref[b, :, :width] = jnp.dot(
            weights.astype(BF), tokens_ref[b], preferred_element_type=F32
        )
        stats = jnp.zeros((slots, STAT), F32)
        for j, part in enumerate(pieces(peak) + pieces(total)):
            stats = jnp.where(lane == j, part, stats)
        sums_ref[b, :, width:] = stats
        logits_ref[b] = masked
    for b in range(seqs):
        for out_ref, group in zip(out_refs, groups):
            for j, k in enumerate(group):
                rows = pl.ds(pl.multiple_of(peer(me, k, n_exp) * own, own), own)
                out_ref[j, b * own:(b + 1) * own, :] = sums_ref[b, rows, :].astype(BF)


def weights_kernel(n_exp, own, logits_ref, part_ref, out_ref, part_out_ref, weights_ref, rel_ref):
    part_out_ref[...] = part_ref[...]
    seqs, slots, block = logits_ref.shape
    me = lax.axis_index("exp")
    rel_ref[...] = jnp.zeros_like(rel_ref)
    for b in range(seqs):
        logits = logits_ref[b]
        dead = logits[:1] < -9e29
        grown = jnp.exp(logits - jnp.max(logits, axis=0, keepdims=True))
        weights = grown / jnp.sum(grown, axis=0, keepdims=True)
        weights_ref[...] = jnp.where(dead, 0.0, weights)
        for k in range(n_exp):
            rows = pl.ds(pl.multiple_of(peer(me, k, n_exp) * own, own), own)
            at = (k * seqs + b) * own
            rel_ref[b, at:at + own, :] = weights_ref[rows, :]
    for b in range(seqs):
        out_ref[b] = rel_ref[b].T.astype(BF)


def merge_kernel(n_exp, *refs):
    parts, outs = refs[:-n_exp - 1], refs[-n_exp:]
    width = outs[0].shape[-1]
    for k in range(n_exp):
        stats = [part[k, :, width:].astype(F32) for part in parts]
        peaks = [s[:, 0:1] + s[:, 1:2] + s[:, 2:3] for s in stats]
        totals = [s[:, 3:4] + s[:, 4:5] + s[:, 5:6] for s in stats]
        top = functools.reduce(jnp.maximum, peaks)
        scales = [jnp.exp(peak - top) for peak in peaks]
        total = sum(t * s for t, s in zip(totals, scales))
        sums = sum(part[k, :, :width].astype(F32) * s for part, s in zip(parts, scales))
        outs[k][...] = (sums / total).astype(BF)


def expert_kernel(n_exp, own, groups, *refs):
    slots = refs[:n_exp]
    first_ref, second_ref, out_ref, in_ref, sum_ref = refs[n_exp:]
    rows = slots[0].shape[0]
    chunks = in_ref.shape[0]
    for k in range(n_exp):
        for c in range(chunks):
            in_ref[c, k * rows:(k + 1) * rows, :] = slots[k][:, c * LANES:(c + 1) * LANES].astype(F32)
    count = n_exp * rows // own
    for s in range(own):
        same = pl.ds(s, count, stride=own)
        mine = jnp.concatenate([in_ref[c, same, :] for c in range(chunks)], axis=1).astype(BF)
        hidden = jnp.dot(mine, first_ref[s], preferred_element_type=F32)
        hidden = (0.5 * hidden * (1.0 + lax.erf(hidden * 0.7071067811865476))).astype(BF)
        partial = jnp.dot(hidden, second_ref[s], preferred_element_type=F32)
        for c in range(chunks):
            sum_ref[c, same, :] = partial[:, c * LANES:(c + 1) * LANES]
    for ref, group in zip(out_ref, groups):
        for j, k in enumerate(group):
            for c in range(chunks):
                ref[j, :, c * LANES:(c + 1) * LANES] = sum_ref[c, k * rows:(k + 1) * rows, :].astype(BF)


def total_kernel(*refs):
    n = refs[0].shape[0]
    parts, outs = refs[:-n], refs[-n:]
    for k in range(n):
        outs[k][...] = sum(part[k].astype(F32) for part in parts).astype(BF)


def copy_kernel(in_ref, out_ref):
    out_ref[...] = in_ref[...]


def combine_kernel(*refs):
    weights_ref, out_hbm, out_ref, done, parts = refs[0], refs[-3], refs[-2], refs[-1], refs[1:-3]
    seqs, block, _ = out_ref.shape
    step = block // 4
    slot_out = jnp.concatenate([part[...] for part in parts], axis=0)
    copies = []
    for b in range(seqs):
        for j in range(4):
            rows = slice(j * step, (j + 1) * step)
            mixed = jnp.dot(weights_ref[b, rows, :], slot_out, preferred_element_type=F32)
            out_ref[b, rows, :] = mixed.astype(BF)
            at = b * 4 + j
            copies.append(pltpu.make_async_copy(out_ref.at[b, rows], out_hbm.at[b, rows], done.at[at]))
            copies[-1].start()
    for copy in copies:
        copy.wait()


def call(kernel, outs, scratch, limit, flops=0, moved=0):
    return pl.pallas_call(
        kernel,
        out_shape=outs,
        scratch_shapes=scratch,
        compiler_params=pltpu.CompilerParams(vmem_limit_bytes=limit),
        cost_estimate=pl.CostEstimate(flops=flops, bytes_accessed=moved, transcendentals=0),
    )


def shards(tokens, router, image_counts, image_offsets, expert_in, expert_out):
    n_tok, n_exp = lax.axis_size("tok"), lax.axis_size("exp")
    seqs, block, width = tokens.shape
    slots, own = router.shape[1], expert_in.shape[0]
    rows = seqs * own
    S = jax.ShapeDtypeStruct
    limit = max(4 << 20, 8 * n_tok * n_exp * rows * (width + STAT))

    def gather_tok(x, order):
        got = {}
        for k in list(range(1, n_tok))[::order]:
            got[k] = lax.ppermute(x, "tok", [(i, tok_peer(i, k, n_tok)) for i in range(n_tok)])
        return [x] + [got[k] for k in range(1, n_tok)]

    def send(x, k, back):
        if k == 0:
            return x
        pairs = [(i, peer(i, k, n_exp)) for i in range(n_exp)]
        return lax.ppermute(x, "exp", [(b, a) for a, b in pairs] if back else pairs)

    groups = GROUPS(n_exp)
    *parts, logits = pl.pallas_call(
        functools.partial(dispatch_kernel, n_exp, own, groups),
        in_specs=[pl.BlockSpec(memory_space=pltpu.HBM)] * 4,
        out_shape=[S((len(g), rows, width + STAT), BF) for g in groups] + [S((seqs, slots, block), F32)],
        scratch_shapes=[
            pltpu.SMEM(image_counts.shape, jnp.int32),
            pltpu.SMEM(image_offsets.shape, jnp.int32),
            pltpu.VMEM(tokens.shape, BF),
            pltpu.VMEM((slots, width), BF),
            pltpu.VMEM((seqs, slots, width + STAT), F32),
            pltpu.SemaphoreType.DMA((seqs + 3,)),
        ],
        compiler_params=pltpu.CompilerParams(vmem_limit_bytes=WHOLE),
        cost_estimate=pl.CostEstimate(flops=COST_A, bytes_accessed=0, transcendentals=0),
    )(*[pltpu.with_memory_space_constraint(x, pltpu.HBM) for x in (image_counts, image_offsets, tokens, router.T)])
    gathered = [gather_tok(part, TOK_ORDER) for part in parts[:-1]]
    combine_weights, parts[-1] = call(
        functools.partial(weights_kernel, n_exp, own),
        [S((seqs, block, n_exp * rows), BF), S(parts[-1].shape, BF)],
        [pltpu.VMEM((slots, block), F32), pltpu.VMEM((seqs, n_exp * rows, block), F32)],
        4 << 20,
        COST_W,
    )(logits, parts[-1])
    gathered.append(gather_tok(parts[-1], TOK_ORDER))
    arrived = {}
    for group, part in zip(groups, gathered):
        merged = call(
            functools.partial(merge_kernel, len(group)),
            [S((rows, width), BF)] * len(group), [], limit, COST_M,
        )(*part, combine_weights)
        for k, block in zip(group, merged):
            arrived[k] = send(block, k, False)
    arrived = [arrived[k] for k in range(n_exp)]
    partial = call(
        functools.partial(expert_kernel_flat, n_exp, own, groups),
        [S((len(g), rows, width), BF) for g in groups],
        [pltpu.VMEM((width // LANES, n_exp * rows, LANES), F32)] * 2,
        EXPERT_LIMIT,
    )(*arrived, expert_in, expert_out)
    gathered = [gather_tok(part, TOK2_ORDER) for part in partial[:-1]]
    mine = call(copy_kernel, S(partial[-1].shape, BF), [], 1 << 20, COST_C)(partial[-1])
    gathered.append(gather_tok(mine, TOK2_ORDER))
    returned = {}
    for group, part in zip(groups, gathered):
        totals = call(total_kernel, [S((rows, width), BF)] * len(group), [], limit)(*part)
        for k, block_out in zip(group, totals):
            returned[k] = send(block_out, k, True)
    return pl.pallas_call(
        combine_kernel,
        in_specs=[VM] * (1 + n_exp),
        out_specs=ANY,
        out_shape=S(tokens.shape, BF),
        scratch_shapes=[pltpu.VMEM(tokens.shape, BF), pltpu.SemaphoreType.DMA((4 * seqs,))],
        compiler_params=pltpu.CompilerParams(vmem_limit_bytes=limit + (4 << 20)),
    )(combine_weights, *[returned[k] for k in range(n_exp)])


EXPERT_LIMIT = 8 << 20
COST_C = 3_000_000_000
COST_A = 40_000_000_000
COST_W = 6_000_000_000
COST_M = 0_000_000_000


def expert_kernel_flat(n_exp, own, groups, *refs):
    n = len(groups)
    ins, outs, scratch = refs[:n_exp + 2], refs[n_exp + 2:n_exp + 2 + n], refs[n_exp + 2 + n:]
    expert_kernel(n_exp, own, groups, *ins, outs, *scratch)


def solution(mesh):
    placed = (
        P(("dp", "exp"), "tok", None),
        P(None, "dp"),
        P(("dp", "exp"), None),
        P(("dp", "exp"), None),
        P("exp", None, "tok"),
        P("exp", "tok", None),
    )
    return jax.shard_map(
        shards, mesh=mesh, in_specs=placed, out_specs=P(("dp", "exp"), "tok", None), check_vma=False
    )
```
